256 devices in a mesh: row: 16 (over x, z_lo, core), col: 16 (over z_hi, y).
Axes of the slice: x: 4, y: 4, z: 8 (z_hi: 4, z_lo: 2; z = z_hi * 2 + z_lo), core: 2. Of those that a mesh axis runs over, the one named last changes fastest.
Arguments:
- coefs: bfloat16 [1024, 16384], P('col', 'row'), may hold values from -6 to 6
- direction: bfloat16 [1024, 16384], P('col', 'row'), may hold values from -6 to 6
- tiles: bfloat16 [16, 384, 4096], P('row', 'col'), may hold values from -0.21875 to 0.21875
- block_rows: int32 [16, 384], P('row', 'col'), may hold values from 0 to 15
- block_cols: int32 [16, 384], P('row', 'col'), may hold values from 0 to 255
- counts: int32 [16, 16], P('row', 'col'), may hold values from 3 to 24, as said below
Outputs:
- h_coefs: bfloat16 [1024, 16384], P('col', 'row')
- h_direction: bfloat16 [1024, 16384], P('col', 'row')
The draws below stay inside these ranges and needn't reach their ends.
Inputs may be any that keep to these rules, and one draw needn't show every extreme that they name: `counts`: each value lies between 3 and 24; some device's list is full in every draw. `block_cols`: tiles of one device may repeat a place.
All inputs are finite; a program needn't handle non-finite values.
Results may differ from the reference program's by a relative error of at most 0.008.
Values may be sent and summed in bfloat16 or wider, within the bound.
No kernel may reach another device: no remote copies, remote signals or barrier semaphores. Data moves between devices by JAX's collectives and lax.ppermute only.
A program may use at most 128 MiB of HBM per device.

```python
import jax
import jax.numpy as jnp
from jax import lax

BLOCK = 64
ORBS = 1024
RB_DEV = 16
TILES_DEV = 24
NB = 256
NBASIS = 16384
N_ROW = 16
N_COL = 16


def draw_counts(key, part):
    first_key, second_key = jax.random.split(jax.random.fold_in(key, 7))
    lowest = max(1, TILES_DEV // 8)
    values = jax.random.randint(first_key, (N_ROW * N_COL,), lowest, TILES_DEV + 1)
    chosen = jax.random.randint(second_key, (), 0, N_ROW * N_COL)
    values = jnp.where(jnp.arange(N_ROW * N_COL) == chosen, TILES_DEV, values)
    return values.reshape(N_ROW, N_COL).astype(jnp.int32)


def with_ends(array, rng, least, largest):
    spot = [jax.random.randint(jax.random.fold_in(rng, axis), (), 0, length) for axis, length in enumerate(array.shape)]
    longest = array.shape.index(max(array.shape))
    next_to = spot[:longest] + [(spot[longest] + 1) % array.shape[longest]] + spot[longest + 1:]
    return array.at[tuple(spot)].set(least).at[tuple(next_to)].set(largest)


def steps_of(own_key, shape, cuts, smallest, high):
    factor_of, own = 1.0, jax.random.fold_in(own_key, 6)
    for position, blocks in cuts:
        steps = jnp.exp(jax.random.uniform(jax.random.fold_in(own, position), (blocks,), jnp.float32, smallest / len(cuts), high / len(cuts)))
        factor_of = factor_of * jnp.repeat(steps, shape[position] // blocks).reshape([-1 if axis == position else 1 for axis in range(len(shape))])
    return factor_of


def centred(own_key, dims, deviation, bound, cuts=(), kind=jnp.bfloat16):
    array = deviation * jax.random.normal(own_key, dims, jnp.float32)
    if cuts:
        array = array * steps_of(own_key, dims, cuts, -0.22, 0.18)
    return jnp.clip(array, -bound, bound).astype(kind)


def setup_inputs(seed: int = 0) -> dict:
    seeds = jax.random.split(jax.random.key(seed), 7)
    coefs = centred(seeds[0], (ORBS, NBASIS), 1.0, 6.0, ((0, 16), (1, 16)))
    direction = centred(seeds[1], (ORBS, NBASIS), 1.0, 6.0, ((0, 16), (1, 16)))
    tiles = centred(seeds[2], (N_ROW, N_COL * TILES_DEV, BLOCK * BLOCK), (BLOCK * N_COL * TILES_DEV // RB_DEV // 2) ** -0.5, 0.21875, ((0, 16), (1, 16)))
    block_rows = with_ends(jax.random.randint(seeds[3], (N_ROW, N_COL * TILES_DEV), 0, RB_DEV), jax.random.fold_in(seeds[3], 1), 0, RB_DEV - 1).astype(jnp.int32)
    block_cols = with_ends(jax.random.randint(seeds[4], (N_ROW, N_COL * TILES_DEV), 0, NB), jax.random.fold_in(seeds[4], 1), 0, NB - 1).astype(jnp.int32)
    counts = draw_counts(jax.random.fold_in(seeds[6], 71), 0)
    return {"coefs": coefs, "direction": direction, "tiles": tiles, "block_rows": block_rows, "block_cols": block_cols, "counts": counts}


def reference(coefs, direction, tiles, block_rows, block_cols, counts):
    nblocks = RB_DEV * N_ROW
    panels = jnp.stack([coefs, direction]).astype(jnp.float32).reshape(2, ORBS, nblocks, BLOCK)
    slot = jnp.arange(N_COL * TILES_DEV, dtype=jnp.int32)
    owner = slot // TILES_DEV
    within = slot % TILES_DEV
    targets = jnp.arange(RB_DEV, dtype=jnp.int32)

    def group(r):
        valid = within < counts[r][owner]
        mats = jnp.where(valid[:, None], tiles[r].astype(jnp.float32), jnp.float32(0.0))
        mats = mats.reshape(N_COL, TILES_DEV, BLOCK, BLOCK)
        rows_here = block_rows[r].reshape(N_COL, TILES_DEV)
        cols_here = block_cols[r].reshape(N_COL, TILES_DEV)

        def step(total, pieces):
            tile_mats, tile_rows, tile_cols = pieces
            picked = jnp.take(panels, tile_cols, axis=2)
            contrib = jnp.einsum('pij,sopj->psoi', tile_mats, picked).reshape(TILES_DEV, -1)
            onehot = (tile_rows[:, None] == targets[None, :]).astype(jnp.float32)
            return total + jnp.dot(onehot.T, contrib, precision=lax.Precision.HIGHEST, preferred_element_type=jnp.float32), None

        start = jnp.zeros((RB_DEV, 2 * ORBS * BLOCK), jnp.float32)
        total, unused = lax.scan(step, start, (mats, rows_here, cols_here))
        return total

    totals = lax.map(group, jnp.arange(N_ROW, dtype=jnp.int32))
    totals = totals.reshape(N_ROW, RB_DEV, 2, ORBS, BLOCK).transpose(2, 3, 0, 1, 4)
    result = totals.reshape(2, ORBS, nblocks * BLOCK).astype(jnp.bfloat16)
    return result[0], result[1]
```

```python
import jax
import jax.numpy as jnp
from jax import lax
from jax.experimental import pallas as pl
from jax.experimental.pallas import tpu as pltpu
from jax.sharding import PartitionSpec as P

BLOCK = 64
LANES = 128
META = 16

NX, NZ, NC = 4, 2, 2
MX, MY = 4, 4


def row_pairs(move):
    pairs = []
    for x in range(NX):
        for z in range(NZ):
            for c in range(NC):
                a, b, d = move(x, z, c)
                pairs.append(((x * NZ + z) * NC + c, ((a % NX) * NZ + b) * NC + d))
    return pairs


def col_pairs(move):
    pairs = []
    for z in range(MX):
        for y in range(MY):
            a, b = move(z, y)
            pairs.append((z * MY + y, (a % MX) * MY + b % MY))
    return pairs


X_UP = row_pairs(lambda x, z, c: (x + 1, z, c))
X_DOWN = row_pairs(lambda x, z, c: (x - 1, z, c))
Z_SWAP = row_pairs(lambda x, z, c: (x, 1 - z, c))
C_SWAP = row_pairs(lambda x, z, c: (x, z, 1 - c))
Z_UP = col_pairs(lambda z, y: (z + 1, y))
Z_DOWN = col_pairs(lambda z, y: (z - 1, y))
Y_UP = col_pairs(lambda z, y: (z, y + 1))
Y_DOWN = col_pairs(lambda z, y: (z, y - 1))


def pack_kernel(coefs, direction, tiles, rows, cols, counts, panel, packed, wide, pairs):
    slots = tiles.shape[0]
    chunks = tiles.shape[1] // LANES
    orbitals = coefs.shape[0]
    both = jnp.concatenate([coefs[...], direction[...]], axis=0)
    panel[...] = both.T
    for q in range(chunks):
        wide[pl.ds(q, slots, stride=chunks), :] = tiles[:, q * LANES:(q + 1) * LANES].astype(jnp.float32)
    low = lax.broadcasted_iota(jnp.int32, (chunks, LANES), 1) < BLOCK
    for p in range(slots // 2):
        first = wide[2 * p * chunks:(2 * p + 1) * chunks, :]
        second = wide[(2 * p + 1) * chunks:(2 * p + 2) * chunks, :]
        even = jnp.where(low, first, pltpu.roll(second, BLOCK, 1))
        odd = jnp.where(low, pltpu.roll(first, BLOCK, 1), second)
        pairs[pl.ds(p * BLOCK, chunks, stride=2), :] = even
        pairs[pl.ds(p * BLOCK + 1, chunks, stride=2), :] = odd
    base = slots // 2 * BLOCK
    pairs[base:base + META, :] = jnp.zeros((META, LANES), jnp.float32)
    pairs[base:base + 1, 0:slots] = rows[...].astype(jnp.float32)
    pairs[base + 1:base + 2, 0:slots] = cols[...].astype(jnp.float32)
    pairs[base + 2:base + 3, :] = jnp.broadcast_to(counts[...].astype(jnp.float32), (1, LANES))
    packed[...] = pairs[...].astype(jnp.bfloat16)


def pack(coefs, direction, tiles, rows, cols, counts):
    slots = tiles.shape[0]
    length = slots // 2 * BLOCK + META
    return pl.pallas_call(
        pack_kernel,
        out_shape=(
            jax.ShapeDtypeStruct((coefs.shape[1], LANES), jnp.bfloat16),
            jax.ShapeDtypeStruct((length, LANES), jnp.bfloat16),
        ),
        in_specs=[pl.BlockSpec(memory_space=pltpu.VMEM)] * 6,
        out_specs=(pl.BlockSpec(memory_space=pltpu.VMEM),) * 2,
        scratch_shapes=[
            pltpu.VMEM((slots * BLOCK * BLOCK // LANES, LANES), jnp.float32),
            pltpu.VMEM((length, LANES), jnp.float32),
        ],
        name="pack",
    )(coefs, direction, tiles, rows, cols, counts)


GROUP = 4


def apply_kernel(slots, xmoves, *refs):
    nx = len(xmoves)
    panels = refs[:nx]
    lists = refs[nx:2 * nx]
    out_one, out_two = refs[2 * nx:2 * nx + 2]
    whole, held, total, meta, smem, xsem, tsem, msem = refs[2 * nx + 2:]
    me = lax.axis_index("row")
    x, z, c = me // (NZ * NC), me // NC % NZ, me % NC
    depth = panels[0].shape[0] // BLOCK
    length = lists[0].shape[0]
    pairs = slots // 2

    tcopies = [pltpu.make_async_copy(t, held.at[i], tsem.at[i]) for i, t in enumerate(lists)]
    for copy in tcopies:
        copy.start()
    xcopies = []
    for i, (panel, (dx, dz, dc)) in enumerate(zip(panels, xmoves)):
        spot = (lax.rem(x + dx, NX) * NZ + lax.rem(z + dz, NZ)) * NC + lax.rem(c + dc, NC)
        copy = pltpu.make_async_copy(panel, whole.at[pl.ds(spot * depth * BLOCK, depth * BLOCK)], xsem.at[i])
        copy.start()
        xcopies.append(copy)
    total[...] = jnp.zeros_like(total)
    for i, copy in enumerate(tcopies):
        copy.wait()
        block = held[i, length - META:length, :].astype(jnp.float32).astype(jnp.int32)
        meta[i * 8:(i + 1) * 8, :] = block[0:8]
    move = pltpu.make_async_copy(meta, smem, msem)
    move.start()
    for copy in xcopies:
        copy.wait()
    move.wait()
    low = lax.broadcasted_iota(jnp.int32, (BLOCK, LANES), 1) < BLOCK
    rows_out = total.shape[0] // BLOCK - 1

    def per_list(i, carry):
        count = smem[i * 8 + 2, 0]

        def per_group(k, carry):
            for u in range(GROUP):
                p = k * GROUP + u
                a, b = 2 * p, 2 * p + 1
                ra = jnp.where(a < count, smem[i * 8, a], rows_out)
                rb = jnp.where(b < count, smem[i * 8, b], rows_out)
                ca, cb = smem[i * 8 + 1, a], smem[i * 8 + 1, b]
                tile = held[i, pl.ds(pl.multiple_of(p * BLOCK, BLOCK), BLOCK), :]
                zero = jnp.zeros_like(tile)
                left = jnp.concatenate([jnp.where(low, tile, zero), jnp.where(low, zero, tile)], axis=0)
                right = jnp.concatenate([
                    whole[pl.ds(pl.multiple_of(ca * BLOCK, BLOCK), BLOCK), :],
                    whole[pl.ds(pl.multiple_of(cb * BLOCK, BLOCK), BLOCK), :],
                ], axis=0)
                part = jnp.dot(left, right, preferred_element_type=jnp.float32)
                at_a = pl.ds(pl.multiple_of(ra * BLOCK, BLOCK), BLOCK)
                at_b = pl.ds(pl.multiple_of(rb * BLOCK, BLOCK), BLOCK)
                total[at_a, :] += part[:BLOCK]
                total[at_b, :] += part[BLOCK:]
            return carry

        lax.fori_loop(0, (count + 2 * GROUP - 1) // (2 * GROUP), per_group, 0)
        return carry

    lax.fori_loop(0, nx, per_list, 0)
    half = out_one.shape[0]
    for g in range(rows_out * BLOCK // LANES):
        flat = total[g * LANES:(g + 1) * LANES, :].T.astype(jnp.bfloat16)
        out_one[:, g * LANES:(g + 1) * LANES] = flat[:half]
        out_two[:, g * LANES:(g + 1) * LANES] = flat[half:]


def apply(panels, lists, xmoves, slots, orbitals, basis):
    n = len(panels)
    length = lists[0].shape[0]
    import functools
    return pl.pallas_call(
        functools.partial(apply_kernel, slots, xmoves),
        out_shape=(jax.ShapeDtypeStruct((orbitals, basis), jnp.bfloat16),) * 2,
        in_specs=[pl.BlockSpec(memory_space=pl.ANY)] * (2 * n),
        out_specs=(pl.BlockSpec(memory_space=pltpu.VMEM),) * 2,
        scratch_shapes=[
            pltpu.VMEM((n * basis, LANES), jnp.bfloat16),
            pltpu.VMEM((n, length, LANES), jnp.bfloat16),
            pltpu.VMEM((basis + BLOCK, LANES), jnp.float32),
            pltpu.VMEM((n * 8, LANES), jnp.int32),
            pltpu.SMEM((n * 8, LANES), jnp.int32),
            pltpu.SemaphoreType.DMA((n,)),
            pltpu.SemaphoreType.DMA((n,)),
            pltpu.SemaphoreType.DMA,
        ],
        name="apply",
    )(*panels, *lists)


def local(coefs, direction, tiles, block_rows, block_cols, counts):
    panel, packed = pack(coefs, direction, tiles[0], block_rows, block_cols, counts)

    def hop(value, axis, pairs):
        return lax.ppermute(value, axis, pairs)

    beside = hop(panel, "row", Z_SWAP)
    below, above = hop(packed, "col", Z_UP), hop(packed, "col", Z_DOWN)
    far = hop(below, "col", Z_UP)
    panels, xmoves = [], []
    for dz, start in ((0, panel), (1, beside)):
        left, right = hop(start, "row", X_UP), hop(start, "row", X_DOWN)
        across = hop(left, "row", X_UP) if dz == 0 else hop(right, "row", X_DOWN)
        for dx, value in ((0, start), (3, left), (1, right), (2, across)):
            panels += [value, hop(value, "row", C_SWAP)]
            xmoves += [(dx, dz, 0), (dx, dz, 1)]
    lists = []
    for n, start in enumerate((packed, below, above, far)):
        left, right = hop(start, "col", Y_UP), hop(start, "col", Y_DOWN)
        across = hop(left, "col", Y_UP) if n % 2 == 0 else hop(right, "col", Y_DOWN)
        lists += [start, left, right, across]
    return apply(panels, lists, xmoves, tiles.shape[1], coefs.shape[0], coefs.shape[1])


def solution(mesh):
    return jax.shard_map(
        local,
        mesh=mesh,
        in_specs=(
            P("col", "row"),
            P("col", "row"),
            P("row", "col", None),
            P("row", "col"),
            P("row", "col"),
            P("row", "col"),
        ),
        out_specs=(P("col", "row"), P("col", "row")),
        check_vma=False,
    )
```
